32 devices in a mesh: gx: 4 (over z), gy: 8 (over y, x, core).
Axes of the slice: x: 2, y: 2, z: 4, core: 2. Of those that a mesh axis runs over, the one named last changes fastest.
Arguments:
- child_dens: bfloat16 [296, 8192], P(None, ('gx', 'gy')), may hold values from -0.625 to 0.625
- users: int32 [2048], P(('gx', 'gy')), may hold values from 0 to 31
- local_dens: bfloat16 [296, 16384], P(None, ('gx', 'gy')), may hold values from -6 to 6
- live: int32 [32], P(('gx', 'gy')), may hold values from 16 to 128, as said below
- m2l_ops: bfloat16 [296, 2368], replicated, may hold values from -0.125 to 0.125
- m2l_lists: int32 [8, 4096], P(None, ('gx', 'gy')), may hold values from -1 to 143, as said below
- leaf_pos: float32 [3, 131072], P(None, ('gx', 'gy')), may hold values from 0 to 1
- leaf_charge: float32 [4, 131072], P(None, ('gx', 'gy')), may hold values from -0.2 to 0.2
- leaf_nbrs: int32 [4096, 27], P(('gx', 'gy')), may hold values from -1 to 159, as said below
Outputs:
- local_exp: float32 [296, 16384], P(None, ('gx', 'gy'))
- near_pot: float32 [4, 131072], P(None, ('gx', 'gy'))
The draws below stay inside these ranges and needn't reach their ends.
Inputs may be any that keep to these rules, and one draw needn't show every extreme that they name: `live`: at least 16 on every device; some device has exactly 128. `m2l_lists`: entry for target slot k lies in k .. k + 16 or is -1. `leaf_nbrs`: entry for leaf l of a device lies in l .. l + 32 or is -1; the first entry is the leaf itself, l + 16.
All inputs are finite; a program needn't handle non-finite values.
Results may differ from the reference program's by a relative error of at most 0.00071.
Values may be sent and summed in bfloat16 or wider, within the bound.
A program may use at most 128 MiB of HBM per device.

```python
import jax
import jax.numpy as jnp
from jax import lax

P_SIZE = 296
Q = 4
NOFF = 8
OCT_DEV = 128
H = 8
SH_DEV = 1
CH_DEV = 64
LEAF_DEV = 128
NPT = 32
NNB = 27
HL = 16
SHARED = 32
NOCT = 4096
CHILDREN = 2048
LEAVES = 4096
DEVICES = 32


def draw_live(key, part):
    key_base, key_full, key_pick = jax.random.split(jax.random.fold_in(key, 11), 3)
    base = jax.random.randint(key_base, (DEVICES,), OCT_DEV // 8, OCT_DEV // 2 + 1)
    full = jax.random.randint(key_full, (DEVICES,), 0, 16) == 0
    pick = jax.random.randint(key_pick, (), 0, DEVICES)
    full = full | (jnp.arange(DEVICES) == pick)
    return jnp.where(full, OCT_DEV, base).astype(jnp.int32)


def draw_m2l_lists(key, part):
    key_step, key_gap = jax.random.split(jax.random.fold_in(key, 23), 2)
    target = jnp.arange(NOCT, dtype=jnp.int32) % OCT_DEV
    step = jax.random.randint(key_step, (NOFF, NOCT), -H, H + 1)
    source = target[None, :] + H + step
    empty = jax.random.randint(key_gap, (NOFF, NOCT), 0, 8) == 0
    source = jnp.where(empty, -1, source)
    source = source.at[0, 0].set(0)
    source = source.at[0, NOCT - 1].set(OCT_DEV + 2 * H - 1)
    source = source.at[1, 0].set(-1)
    return source.astype(jnp.int32)


def draw_leaf_nbrs(key, part):
    key_step, key_gap = jax.random.split(jax.random.fold_in(key, 37), 2)
    local = jnp.arange(LEAVES, dtype=jnp.int32) % LEAF_DEV
    step = jax.random.randint(key_step, (LEAVES, NNB), -HL, HL + 1)
    source = local[:, None] + HL + step
    empty = jax.random.randint(key_gap, (LEAVES, NNB), 0, 8) == 0
    source = jnp.where(empty, -1, source)
    source = source.at[:, 0].set(local + HL)
    source = source.at[0, 1].set(0)
    source = source.at[LEAVES - 1, 2].set(LEAF_DEV + 2 * HL - 1)
    source = source.at[0, 3].set(-1)
    return source.astype(jnp.int32)


def with_ends(entries, rng, smallest, high):
    longest = entries.shape.index(max(entries.shape))
    spots = []
    for shift in (0, 1):
        where = [jax.random.randint(jax.random.fold_in(rng, axis), (), 0, length) for axis, length in enumerate(entries.shape)]
        where[longest] = (where[longest] + shift) % entries.shape[longest]
        spots.append(tuple(where))
    return entries.at[spots[0]].set(smallest).at[spots[1]].set(high)


def steps_of(rng, shape, pieces, low, largest):
    loudness = 1.0
    for axis_at, blocks in pieces:
        steps = jax.random.uniform(jax.random.fold_in(jax.random.fold_in(rng, 6), axis_at), (blocks,), jnp.float32, low / len(pieces), largest / len(pieces))
        loudness = loudness * jnp.repeat(jnp.exp(steps), shape[axis_at] // blocks).reshape((-1,) + (1,) * (len(shape) - 1 - axis_at))
    return loudness


def gaussian(rng, extent, scale, most, shards=(), held_as=jnp.bfloat16):
    factor_of = steps_of(rng, extent, shards, -0.22, 0.18) if shards else 1.0
    entries = jax.random.normal(rng, extent, jnp.float32) * scale * factor_of
    return jnp.minimum(jnp.maximum(entries, -most), most).astype(held_as)


def setup_inputs(seed: int = 0) -> dict:
    splits = jax.random.split(jax.random.key(seed), 10)
    return {
        "child_dens": gaussian(splits[0], (P_SIZE, CHILDREN * Q), 0.04, 0.625, ((1, 32),)),
        "users": with_ends(jax.random.randint(splits[1], (CHILDREN,), 0, SHARED), jax.random.fold_in(splits[1], 1), 0, SHARED - 1).astype(jnp.int32),
        "local_dens": gaussian(splits[2], (P_SIZE, NOCT * Q), 1.0, 6.0, ((1, 32),)),
        "live": draw_live(jax.random.fold_in(splits[9], 71), 0),
        "m2l_ops": gaussian(splits[4], (P_SIZE, NOFF * P_SIZE), (NOFF * P_SIZE) ** -0.5, 0.125),
        "m2l_lists": draw_m2l_lists(jax.random.fold_in(splits[9], 71), 0),
        "leaf_pos": jnp.clip(1.0 * jax.random.uniform(splits[6], (3, LEAVES * NPT), jnp.float32) ** steps_of(splits[6], (3, LEAVES * NPT), ((1, 32),), -0.2, 0.2), 0.0, 1.0),
        "leaf_charge": gaussian(splits[7], (Q, LEAVES * NPT), 0.03, 0.2, ((1, 32),), jnp.float32),
        "leaf_nbrs": draw_leaf_nbrs(jax.random.fold_in(splits[9], 71), 0),
    }


soften = 0.01

def alive_slots(count):
    slot = jnp.arange(OCT_DEV, dtype=jnp.int32)
    lower = count // 2
    upper = count - lower
    return (slot < lower) | (slot >= OCT_DEV - upper)

def m2l_device(window, ops_blocks, lists):
    span = window.shape[1]
    extended = jnp.concatenate([window, jnp.zeros((window.shape[0], 1, window.shape[2]), jnp.float32)], axis=1)
    index = jnp.where(lists < 0, span, lists).astype(jnp.int32)
    gathered = jnp.take(extended, index, axis=1)
    return jnp.einsum('ioj,jotq->itq', ops_blocks, gathered, precision=lax.Precision.HIGHEST)

def near_device(window, nbrs):
    span = window.shape[1]
    extended = jnp.concatenate([window, jnp.zeros((window.shape[0], 1, window.shape[2]), jnp.float32)], axis=1)
    index = jnp.where(nbrs < 0, span, nbrs).astype(jnp.int32)
    source = jnp.take(extended, index, axis=1)
    source = source.reshape(source.shape[0], source.shape[1], -1)
    target = window[:3, HL:HL + LEAF_DEV, :]
    dist_sq = jnp.zeros((LEAF_DEV, NPT, source.shape[2]), jnp.float32)
    for coord in range(3):
        diff = target[coord][:, :, None] - source[coord][:, None, :]
        dist_sq = dist_sq + diff * diff
    kernel = 1.0 / jnp.sqrt(dist_sq + soften)
    return jnp.einsum('lts,qls->qlt', kernel, source[3:], precision=lax.Precision.HIGHEST)

def reference(child_dens, users, local_dens, live, m2l_ops, m2l_lists, leaf_pos, leaf_charge, leaf_nbrs):
    child_blocks = jnp.transpose(child_dens.reshape(P_SIZE, DEVICES, CH_DEV, Q), (1, 2, 0, 3))
    user_blocks = users.reshape(DEVICES, CH_DEV)

    def add_device(total, item):
        block, targets = item
        part_sum = jax.ops.segment_sum(block.astype(jnp.float32), targets, num_segments=SHARED)
        return (total + part_sum, jnp.float32(0.0))
    shared, unused = lax.scan(add_device, jnp.zeros((SHARED, P_SIZE, Q), jnp.float32), (child_blocks, user_blocks))
    shared = jnp.transpose(shared.reshape(DEVICES, SH_DEV, P_SIZE, Q), (2, 0, 1, 3))
    own = local_dens.astype(jnp.float32).reshape(P_SIZE, DEVICES, OCT_DEV, Q)
    own = own.at[:, :, :SH_DEV, :].add(shared)
    alive = jax.vmap(alive_slots)(live)
    owned = jnp.where(alive[None, :, :, None], own, jnp.float32(0.0)).astype(jnp.bfloat16)
    padded = jnp.pad(owned.astype(jnp.float32).reshape(P_SIZE, NOCT, Q), ((0, 0), (H, H), (0, 0)))
    ops_blocks = m2l_ops.astype(jnp.float32).reshape(P_SIZE, NOFF, P_SIZE)
    lists_dev = jnp.transpose(m2l_lists.reshape(NOFF, DEVICES, OCT_DEV), (1, 0, 2))
    points = jnp.concatenate([leaf_pos, leaf_charge], axis=0).reshape(3 + Q, LEAVES, NPT)
    points_padded = jnp.pad(points, ((0, 0), (HL, HL), (0, 0)))
    nbrs_dev = leaf_nbrs.reshape(DEVICES, LEAF_DEV, NNB)
    ranks = jnp.arange(DEVICES, dtype=jnp.int32)

    def per_device(item):
        rank, lists, nbrs, count = item
        window = lax.dynamic_slice_in_dim(padded, rank * OCT_DEV, OCT_DEV + 2 * H, axis=1)
        expansion = m2l_device(window, ops_blocks, lists)
        keep = alive_slots(count)
        expansion = jnp.where(keep[None, :, None], expansion, jnp.float32(0.0))
        leaves = lax.dynamic_slice_in_dim(points_padded, rank * LEAF_DEV, LEAF_DEV + 2 * HL, axis=1)
        return (expansion, near_device(leaves, nbrs))
    expansions, nears = lax.map(per_device, (ranks, lists_dev, nbrs_dev, live))
    local_exp = jnp.transpose(expansions, (1, 0, 2, 3)).reshape(P_SIZE, NOCT * Q)
    near_pot = jnp.transpose(nears, (1, 0, 2, 3)).reshape(Q, LEAVES * NPT)
    return (local_exp, near_pot)
```

```python
import functools

import jax
import jax.numpy as jnp
from jax import lax
from jax.experimental import pallas as pl
from jax.experimental.pallas import tpu as pltpu
from jax.sharding import PartitionSpec as P

Q = 4
NOFF = 8
SH_DEV = 1
NPT = 32
HL = 16
GROUP = 8
BLOCK = 32

soften = 0.01
f32 = jnp.float32
bf16 = jnp.bfloat16
MESH = pl.DeviceIdType.MESH


def split3(value):
    first = value.astype(bf16).astype(f32)
    rest = value - first
    second = rest.astype(bf16).astype(f32)
    return first, second, rest - second


def row_ids(shape):
    return lax.broadcasted_iota(jnp.int32, shape, 0)


def lane_ids(shape):
    return lax.broadcasted_iota(jnp.int32, shape, 1)


def with_norm(coords):
    norm = jnp.sum(coords * coords, axis=0, keepdims=True)
    return jnp.where(row_ids(coords.shape) == 3, norm, coords), norm


def source_rows(coords):
    value, _ = with_norm(coords)
    one, two, three = split3(value)
    flat = jnp.where(row_ids(value.shape) < 3, f32(1.0), f32(0.0))
    return jnp.concatenate(
        [one, two, three, one, two, one, flat, jnp.zeros_like(one)], axis=0
    ).astype(bf16)


def target_rows(coords):
    value, norm = with_norm(coords)
    one, two, three = split3(value)
    row = row_ids(value.shape)
    main = jnp.where(row < 3, -2.0 * one, jnp.where(row == 3, f32(1.0), f32(0.0)))
    second = jnp.where(row < 3, -2.0 * two, f32(0.0))
    third = jnp.where(row < 3, -2.0 * three, f32(0.0))
    part = split3(norm + soften)
    flat = jnp.where(
        row == 0,
        part[0],
        jnp.where(row == 1, part[1], jnp.where(row == 2, part[2], f32(0.0))),
    )
    return jnp.concatenate(
        [main, main, main, second, second, third, flat, jnp.zeros_like(one)], axis=0
    ).astype(bf16)


def near_counts(nbrs, counts):
    slots, leaves = nbrs.shape
    groups, eight, reach = counts.shape
    span = GROUP + 2 * HL
    rows = -(-span // 16) * 16
    base = nbrs - lane_ids(nbrs.shape) // GROUP * GROUP
    base = jnp.where(nbrs < 0, -1, base)
    ids = row_ids((rows, leaves))
    total = jnp.zeros((rows, leaves), f32)
    for j in range(slots):
        total = total + jnp.where(ids == base[j : j + 1, :], f32(1.0), f32(0.0))
    spread = row_ids((rows, reach)) == lane_ids((rows, reach)) // NPT
    full = lax.dot_general(
        total.T.astype(bf16),
        jnp.where(spread, f32(1.0), f32(0.0)).astype(bf16),
        (((1,), (0,)), ((), ())),
        preferred_element_type=f32,
    )
    counts[...] = full.reshape(groups, eight, reach)


def near_group(g, sources, targets, charges, counts, out):
    reach = counts.shape[2]
    size = GROUP * NPT
    rows = Q * GROUP
    start = pl.multiple_of(g * size, size)
    right = targets[:, pl.ds(start, size)]
    cnt = counts[g]
    ch = charges[:, pl.ds(start, reach)]
    w = jnp.concatenate([cnt * ch[q : q + 1] for q in range(Q)], axis=0)
    wh = w.astype(bf16)
    wl = (w - wh.astype(f32)).astype(bf16)
    w = jnp.concatenate([wh, wl], axis=0)
    total = jnp.zeros((2 * rows, size), f32)
    for at in range(0, reach, 256):
        width = min(256, reach - at)
        left = sources[pl.ds(pl.multiple_of(start + at, size), width), :]
        kernel = lax.rsqrt(jnp.dot(left, right, preferred_element_type=f32))
        high = kernel.astype(bf16)
        low = (kernel - high.astype(f32)).astype(bf16)
        span = slice(at, at + width)
        total = total + jnp.dot(w[:, span], high, preferred_element_type=f32)
        total = total + jnp.dot(w[:, span], low, preferred_element_type=f32)
    flat = total[:rows] + total[rows:]
    mine = row_ids(flat.shape) % GROUP == lane_ids(flat.shape) // NPT
    flat = jnp.where(mine, flat, f32(0.0))
    out[:, pl.ds(start, size)] = jnp.sum(flat.reshape(Q, GROUP, size), axis=1)


def alive_lanes(live, slots, shape):
    slot = lane_ids(shape) // Q
    lower = live // 2
    return (slot < lower) | (slot >= slots - (live - lower))


def m2l_gather(window, lists, gathered):
    offsets, slots = lists.shape
    surface = window.shape[0]
    wide = slots * Q
    expand = row_ids((slots, wide)) == lane_ids((slots, wide)) // Q
    place = jnp.dot(
        (lists + 1).astype(f32).astype(bf16),
        jnp.where(expand, f32(1.0), f32(0.0)).astype(bf16),
        preferred_element_type=f32,
    ).astype(jnp.int32)
    place = (place - 1) * Q + lane_ids(place.shape) % Q
    size = BLOCK * Q
    depth = (BLOCK + slots // 8) * Q
    for b in range(slots // BLOCK):
        block = window[:, b * size : b * size + depth]
        ids = row_ids((depth, size)) + b * size
        for o in range(0, offsets, 2):
            hits = [
                ids == place[k : k + 1, b * size : (b + 1) * size] for k in (o, o + 1)
            ]
            hot = jnp.concatenate([jnp.where(hit, f32(1.0), f32(0.0)) for hit in hits], axis=1)
            pair = jnp.dot(block, hot.astype(bf16), preferred_element_type=f32)
            both = jnp.concatenate([pair[:, :size], pair[:, size:]], axis=0).astype(bf16)
            gathered[o * surface : (o + 2) * surface, b * size : (b + 1) * size] = both


def partial_sums(child, users, send, nx, ny):
    own = SH_DEV * Q
    rows = send.shape[0]
    chunks, count = users.shape
    wide = count * Q
    row = row_ids((rows, wide))
    owner = row // own % nx * ny + row // (own * nx)
    target = owner * own + row % own
    expand = row_ids((count, wide)) == lane_ids((count, wide)) // Q
    expand = jnp.where(expand, f32(1.0), f32(0.0)).astype(bf16)

    def chunk_sum(i):
        ids = users[pl.ds(i, 1), :]
        both = jnp.concatenate([ids // 256, ids % 256], axis=0)
        both = jnp.concatenate([both, both, both, both], axis=0)
        place = jnp.dot(
            both.astype(f32).astype(bf16), expand, preferred_element_type=f32
        ).astype(jnp.int32)
        place = (place[0:1] * 256 + place[1:2]) * Q + lane_ids((1, wide)) % Q
        hot = jnp.where(target == place, f32(1.0), f32(0.0)).astype(bf16)
        block = child[:, pl.ds(pl.multiple_of(i * wide, wide), wide)]
        return lax.dot_general(
            hot, block, (((1,), (1,)), ((), ())), preferred_element_type=f32
        )

    send[...] = chunk_sum(0)
    if chunks > 1:

        def step(i, carry):
            send[...] += chunk_sum(i)
            return carry

        lax.fori_loop(1, chunks, step, 0)


def fused_kernel(
    nx,
    ny,
    live_in,
    child_in,
    users_in,
    local_in,
    pos_in,
    charge_in,
    nbrs_in,
    lists_in,
    ops_in,
    window,
    out,
    lists,
    ops,
    live,
    child,
    users,
    local,
    pos,
    charge,
    nbrs,
    send1,
    recv1,
    send2,
    recv2,
    recv3,
    spread,
    first,
    last,
    low,
    high,
    pos_low,
    pos_high,
    charge_low,
    charge_high,
    coords,
    charges,
    sources,
    targets,
    counts,
    load_sem,
    send_sem,
    recv_sem,
):
    mx, my = lax.axis_index("gx"), lax.axis_index("gy")
    total = nx * ny
    me = mx * ny + my
    has_low = me > 0
    has_high = me < total - 1

    def place(rank):
        return rank // ny, lax.rem(rank, ny)

    after = place(lax.rem(me + 1, total))
    before = place(lax.rem(me + total - 1, total))
    along_y = [(mx, lax.rem(my + d, ny)) for d in range(1, ny)]
    along_x = [(lax.rem(mx + d, nx), my) for d in range(1, nx)]

    barrier = pltpu.get_barrier_semaphore()

    def greet(device):
        pl.semaphore_signal(barrier, inc=1, device_id=device, device_id_type=MESH)

    for device in along_x + along_y:
        greet(device)
    pl.when(has_low)(lambda: greet(before))
    pl.when(has_high)(lambda: greet(after))

    def load(k, src, dst):
        copy = pltpu.make_async_copy(src, dst, load_sem.at[k])
        copy.start()
        return copy

    load_child = [load(0, child_in, child), load(1, users_in, users)]
    load_leaf = [load(2, pos_in, pos), load(3, charge_in, charge), load(4, nbrs_in, nbrs)]
    load_local = [load(5, local_in, local), load(6, live_in, live)]
    load_ops = [load(7, lists_in, lists), load(8, ops_in, ops)]

    surface, wide = local.shape
    slots = wide // Q
    rim = low.shape[1]
    halo = pos_low.shape[1]
    count = pos.shape[1]
    own = SH_DEV * Q
    message = nx * own
    for copy in load_child:
        copy.wait()
    partial_sums(child, users, send1, nx, ny)
    for copy in load_leaf:
        copy.wait()
    coords[...] = jnp.zeros_like(coords)
    coords[0:3, halo : halo + count] = pos[...]
    charges[:, halo : halo + count] = charge[...]
    mine = coords[:, halo : halo + count]
    sources[halo : halo + count, :] = source_rows(mine).T
    targets[...] = target_rows(mine)
    near_counts(nbrs[...], counts)
    for copy in load_local:
        copy.wait()
    last[...] = local[:, wide - rim :]
    first[...] = local[:, 0:rim]

    groups = counts.shape[0]
    skip = halo // (GROUP * NPT)
    pairs = (groups - 2 * skip) // 2

    def step(p, carry):
        for g in range(2):
            near_group(skip + 2 * p + g, sources, targets, charges, counts, out)
        return carry

    early = jnp.where(me == 0, 3, jnp.where(me == 1, 2, jnp.where(me < ny, 1, 0)))
    early = jnp.minimum(early, pairs)
    half = jnp.minimum(early + (pairs + 1) // 2, pairs)
    lax.fori_loop(0, early, step, 0)
    neighbours = jnp.where(has_low, 1, 0) + jnp.where(has_high, 1, 0)
    pl.semaphore_wait(barrier, len(along_y) + len(along_x) + neighbours)

    at = [0]

    def remote(src, dst, device, sends=None, takes=None):
        k = at[0]
        at[0] += 1
        copy = pltpu.make_async_remote_copy(
            src_ref=src,
            dst_ref=dst,
            send_sem=send_sem.at[k],
            recv_sem=recv_sem.at[k],
            device_id=device,
            device_id_type=MESH,
        )
        if sends is None:
            copy.start()
            return copy.wait
        pl.when(sends)(copy.start)

        def wait():
            pl.when(sends)(copy.wait_send)
            pl.when(takes)(copy.wait_recv)

        return wait

    step1 = []
    for d in range(1, ny):
        start = pl.multiple_of(lax.rem(my + d, ny) * message, message)
        step1.append(
            remote(send1.at[pl.ds(start, message), :], recv1.at[d - 1], along_y[d - 1])
        )
    leaf = [
        remote(pos.at[:, count - halo : count], pos_low, after, has_high, has_low),
        remote(charge.at[:, count - halo : count], charge_low, after, has_high, has_low),
        remote(pos.at[:, 0:halo], pos_high, before, has_low, has_high),
        remote(charge.at[:, 0:halo], charge_high, before, has_low, has_high),
    ]
    rims = [
        remote(last, low, after, has_high, has_low),
        remote(first, high, before, has_low, has_high),
    ]

    lax.fori_loop(early, half, step, 0)

    for wait in step1:
        wait()
    value = send1[pl.ds(pl.multiple_of(my * message, message), message), :]
    for d in range(ny - 1):
        value = value + recv1[d]
    for k in range(nx):
        send2[k] = value[k * own : (k + 1) * own]
    step2 = []
    for d in range(nx):
        row = lax.rem(mx + d, nx)
        rank = row * ny + my
        left = place(lax.rem(rank + total - 1, total))
        step2.append(remote(send2.at[row], recv3.at[d], left, rank > 0, has_high))
        if d > 0:
            step2.append(remote(send2.at[row], recv2.at[d - 1], along_x[d - 1]))

    lax.fori_loop(half, pairs, step, 0)

    alive = alive_lanes(live[...], slots, (surface, wide))
    owned = jnp.where(alive, local[...].astype(f32), f32(0.0))
    lanes = spread.shape[0]
    window[:, rim + lanes : rim + wide] = owned[:, lanes:].astype(bf16)

    for wait in leaf:
        wait()
    for pos_ref, charge_ref, start, there in (
        (pos_low, charge_low, 0, has_low),
        (pos_high, charge_high, halo + count, has_high),
    ):
        span = slice(start, start + halo)
        coords[0:3, span] = jnp.where(there, pos_ref[...], f32(0.0))
        charges[:, span] = jnp.where(there, charge_ref[...], f32(0.0))
        sources[span, :] = source_rows(coords[:, span]).T

    def edge(p, carry):
        for g in range(2):
            at_low = 2 * p + g
            g = jnp.where(at_low < skip, at_low, groups - 2 * skip + at_low)
            near_group(g, sources, targets, charges, counts, out)
        return carry

    lax.fori_loop(0, skip, edge, 0)

    for copy in load_ops:
        copy.wait()
    for wait in rims:
        wait()
    window[:, 0:rim] = jnp.where(has_low, low[...], jnp.zeros_like(low))
    for wait in step2:
        wait()
    shared = send2[mx]
    for d in range(nx - 1):
        shared = shared + recv2[d]
    spread[...] = jnp.zeros_like(spread)
    spread[0:own, :] = shared
    front = owned[:, 0:lanes] + spread[...].T
    front = jnp.where(alive[:, 0:lanes], front, f32(0.0)).astype(bf16)
    window[:, rim : rim + lanes] = front
    shared = recv3[0]
    for d in range(1, nx):
        shared = shared + recv3[d]
    spread[0:own, :] = shared
    front = high[...].astype(f32) + spread[...].T[:, 0:rim]
    window[:, rim + wide :] = jnp.where(has_high, front, f32(0.0)).astype(bf16)


def fused(live, child, users, local, pos, charge, nbrs, lists, ops):
    nx, ny = lax.axis_size("gx"), lax.axis_size("gy")
    users = users.reshape(-1, 64)
    nbrs = nbrs.T
    live = live.reshape(1, 1)
    surface, wide = local.shape
    count = pos.shape[1]
    halo = HL * NPT
    groups = count // NPT // GROUP
    span = count + 2 * halo
    reach = (GROUP + 2 * HL) * NPT
    rim = wide // 16
    own = SH_DEV * Q
    copies = ny - 1 + 2 * nx - 1 + 6
    vmem = pl.BlockSpec(memory_space=pltpu.VMEM)
    inputs = (live, child, users, local, pos, charge, nbrs, lists, ops)
    inputs = [live] + [pltpu.with_memory_space_constraint(x, pltpu.HBM) for x in inputs[1:]]
    return pl.pallas_call(
        functools.partial(fused_kernel, nx, ny),
        out_shape=(
            jax.ShapeDtypeStruct((surface, wide + 2 * rim), bf16),
            jax.ShapeDtypeStruct(charge.shape, f32),
            jax.ShapeDtypeStruct(lists.shape, lists.dtype),
            jax.ShapeDtypeStruct(ops.shape, ops.dtype),
        ),
        in_specs=[pl.BlockSpec(memory_space=pltpu.HBM)] * len(inputs),
        out_specs=(vmem,) * 4,
        scratch_shapes=[pltpu.VMEM(x.shape, x.dtype) for x in inputs[:7]]
        + [
            pltpu.VMEM((ny * nx * own, surface), f32),
            pltpu.VMEM((ny - 1, nx * own, surface), f32),
            pltpu.VMEM((nx, own, surface), f32),
            pltpu.VMEM((nx - 1, own, surface), f32),
            pltpu.VMEM((nx, own, surface), f32),
            pltpu.VMEM((128, surface), f32),
            pltpu.VMEM((surface, rim), bf16),
            pltpu.VMEM((surface, rim), bf16),
            pltpu.VMEM((surface, rim), bf16),
            pltpu.VMEM((surface, rim), bf16),
            pltpu.VMEM((3, halo), f32),
            pltpu.VMEM((3, halo), f32),
            pltpu.VMEM((Q, halo), f32),
            pltpu.VMEM((Q, halo), f32),
            pltpu.VMEM((8, span), f32),
            pltpu.VMEM((Q, span), f32),
            pltpu.VMEM((span, 64), bf16),
            pltpu.VMEM((64, count), bf16),
            pltpu.VMEM((groups, GROUP, reach), f32),
            pltpu.SemaphoreType.DMA((len(inputs),)),
            pltpu.SemaphoreType.DMA((copies,)),
            pltpu.SemaphoreType.DMA((copies,)),
        ],
        compiler_params=pltpu.CompilerParams(
            collective_id=0, has_side_effects=True, vmem_limit_bytes=32 * 2**20
        ),
    )(*inputs)


def m2l_kernel(live, window, lists, ops, near, out, near_out, gathered, result, sem):
    send = pltpu.make_async_copy(near, near_out, sem.at[0])
    send.start()
    m2l_gather(window, lists[...], gathered)
    surface, wide = result.shape
    alive = alive_lanes(live[...], lists.shape[1], result.shape)
    copies = [send]
    for k in range(2):
        part = slice(k * wide // 2, (k + 1) * wide // 2)
        value = jnp.dot(ops[...], gathered[:, part], preferred_element_type=f32)
        result[:, part] = jnp.where(alive[:, part], value, f32(0.0))
        copy = pltpu.make_async_copy(result.at[:, part], out.at[:, part], sem.at[1 + k])
        copy.start()
        copies.append(copy)
    for copy in copies:
        copy.wait()


def m2l(live, window, lists, ops, near):
    surface = window.shape[0]
    wide = lists.shape[1] * Q
    vmem = pl.BlockSpec(memory_space=pltpu.VMEM)
    hbm = pl.BlockSpec(memory_space=pltpu.HBM)
    return pl.pallas_call(
        m2l_kernel,
        out_shape=(
            jax.ShapeDtypeStruct((surface, wide), f32),
            jax.ShapeDtypeStruct(near.shape, f32),
        ),
        in_specs=[vmem] * 5,
        out_specs=(hbm, hbm),
        scratch_shapes=[
            pltpu.VMEM((surface * lists.shape[0], wide), bf16),
            pltpu.VMEM((surface, wide), f32),
            pltpu.SemaphoreType.DMA((3,)),
        ],
        compiler_params=pltpu.CompilerParams(vmem_limit_bytes=24 * 2**20),
    )(live.reshape(1, 1), window, lists, ops, near)


def per_device(
    child_dens, users, local_dens, live, m2l_ops, m2l_lists, leaf_pos, leaf_charge, leaf_nbrs
):
    window, near_pot, lists, ops = fused(
        live, child_dens, users, local_dens, leaf_pos, leaf_charge, leaf_nbrs, m2l_lists, m2l_ops
    )
    return m2l(live, window, lists, ops, near_pot)


def solution(mesh):
    placed = (
        P(None, ("gx", "gy")),
        P(("gx", "gy")),
        P(None, ("gx", "gy")),
        P(("gx", "gy")),
        P(),
        P(None, ("gx", "gy")),
        P(None, ("gx", "gy")),
        P(None, ("gx", "gy")),
        P(("gx", "gy"), None),
    )
    return jax.shard_map(
        per_device,
        mesh=mesh,
        in_specs=placed,
        out_specs=(P(None, ("gx", "gy")), P(None, ("gx", "gy"))),
        check_vma=False,
    )
```

```python
import functools

import jax
import jax.numpy as jnp
from jax import lax
from jax.experimental import pallas as pl
from jax.experimental.pallas import tpu as pltpu
from jax.sharding import PartitionSpec as P

Q = 4
NOFF = 8
SH_DEV = 1
NPT = 32
HL = 16
GROUP = 8
BLOCK = 32
LANES = 128

soften = 0.01
f32 = jnp.float32
bf16 = jnp.bfloat16
MESH = pl.DeviceIdType.MESH


def split3(value):
    first = value.astype(bf16).astype(f32)
    rest = value - first
    second = rest.astype(bf16).astype(f32)
    return first, second, rest - second


def row_ids(shape):
    return lax.broadcasted_iota(jnp.int32, shape, 0)


def lane_ids(shape):
    return lax.broadcasted_iota(jnp.int32, shape, 1)


def with_norm(coords):
    norm = jnp.sum(coords * coords, axis=0, keepdims=True)
    return jnp.where(row_ids(coords.shape) == 3, norm, coords), norm


def source_rows(coords):
    value, _ = with_norm(coords)
    one, two, three = split3(value)
    flat = jnp.where(row_ids(value.shape) < 3, f32(1.0), f32(0.0))
    return jnp.concatenate(
        [one, two, three, one, two, one, flat, jnp.zeros_like(one)], axis=0
    ).astype(bf16)


def target_rows(coords):
    value, norm = with_norm(coords)
    one, two, three = split3(value)
    row = row_ids(value.shape)
    main = jnp.where(row < 3, -2.0 * one, jnp.where(row == 3, f32(1.0), f32(0.0)))
    second = jnp.where(row < 3, -2.0 * two, f32(0.0))
    third = jnp.where(row < 3, -2.0 * three, f32(0.0))
    part = split3(norm + soften)
    flat = jnp.where(
        row == 0,
        part[0],
        jnp.where(row == 1, part[1], jnp.where(row == 2, part[2], f32(0.0))),
    )
    return jnp.concatenate(
        [main, main, main, second, second, third, flat, jnp.zeros_like(one)], axis=0
    ).astype(bf16)


def near_counts(nbrs, counts):
    slots, leaves = nbrs.shape
    groups, eight, reach = counts.shape
    span = GROUP + 2 * HL
    rows = -(-span // 16) * 16
    base = nbrs - lane_ids(nbrs.shape) // GROUP * GROUP
    base = jnp.where(nbrs < 0, -1, base)
    ids = row_ids((rows, leaves))
    total = jnp.zeros((rows, leaves), f32)
    for j in range(slots):
        total = total + jnp.where(ids == base[j : j + 1, :], f32(1.0), f32(0.0))
    spread = row_ids((rows, reach)) == lane_ids((rows, reach)) // NPT
    full = lax.dot_general(
        total.T.astype(bf16),
        jnp.where(spread, f32(1.0), f32(0.0)).astype(bf16),
        (((1,), (0,)), ((), ())),
        preferred_element_type=f32,
    )
    counts[...] = full.reshape(groups, eight, reach)


def near_group(g, sources, targets, charges, counts, out):
    reach = counts.shape[2]
    size = GROUP * NPT
    rows = Q * GROUP
    start = pl.multiple_of(g * size, size)
    right = targets[:, pl.ds(start, size)]
    cnt = counts[g]
    ch = charges[:, pl.ds(start, reach)]
    w = jnp.concatenate([cnt * ch[q : q + 1] for q in range(Q)], axis=0)
    wh = w.astype(bf16)
    wl = (w - wh.astype(f32)).astype(bf16)
    w = jnp.concatenate([wh, wl], axis=0)
    total = jnp.zeros((2 * rows, size), f32)
    rest = jnp.zeros((rows, size), f32)
    for at in range(0, reach, 256):
        width = min(256, reach - at)
        left = sources[pl.ds(pl.multiple_of(start + at, size), width), :]
        kernel = lax.rsqrt(jnp.dot(left, right, preferred_element_type=f32))
        high = kernel.astype(bf16)
        low = (kernel - high.astype(f32)).astype(bf16)
        span = slice(at, at + width)
        total = total + jnp.dot(w[:, span], high, preferred_element_type=f32)
        rest = rest + jnp.dot(wh[:, span], low, preferred_element_type=f32)
    flat = total[:rows] + total[rows:] + rest
    mine = row_ids(flat.shape) % GROUP == lane_ids(flat.shape) // NPT
    flat = jnp.where(mine, flat, f32(0.0))
    out[:, pl.ds(start, size)] = jnp.sum(flat.reshape(Q, GROUP, size), axis=1)


def alive_lanes(live, slots, shape):
    slot = lane_ids(shape) // Q
    lower = live // 2
    return (slot < lower) | (slot >= slots - (live - lower))


def m2l_gather(window, lists, gathered, blocks):
    offsets, slots = lists.shape
    surface = window.shape[0]
    wide = slots * Q
    expand = row_ids((slots, wide)) == lane_ids((slots, wide)) // Q
    place = jnp.dot(
        (lists + 1).astype(f32).astype(bf16),
        jnp.where(expand, f32(1.0), f32(0.0)).astype(bf16),
        preferred_element_type=f32,
    ).astype(jnp.int32)
    place = (place - 1) * Q + lane_ids(place.shape) % Q
    size = BLOCK * Q
    depth = (BLOCK + slots // 8) * Q
    for i, b in enumerate(blocks):
        block = window[:, b * size : b * size + depth]
        ids = row_ids((depth, size)) + b * size
        for o in range(0, offsets, 2):
            hits = [
                ids == place[k : k + 1, b * size : (b + 1) * size] for k in (o, o + 1)
            ]
            hot = jnp.concatenate([jnp.where(hit, f32(1.0), f32(0.0)) for hit in hits], axis=1)
            pair = jnp.dot(block, hot.astype(bf16), preferred_element_type=f32)
            both = jnp.concatenate([pair[:, :size], pair[:, size:]], axis=0).astype(bf16)
            gathered[o * surface : (o + 2) * surface, i * size : (i + 1) * size] = both


def packed_rows(message, surface):
    whole = surface // LANES
    tail = surface - whole * LANES
    assert tail <= LANES // 2
    return whole * message + (message // 2 if tail else 0)


def unpack(value, message, surface):
    whole = surface // LANES
    tail = surface - whole * LANES
    parts = [value[c * message : (c + 1) * message] for c in range(whole)]
    if tail:
        end = value[whole * message :]
        middle = LANES // 2
        parts.append(jnp.concatenate([end[:, :tail], end[:, middle : middle + tail]], axis=0))
    return jnp.concatenate(parts, axis=1)


def partial_sums(child, users, total, send, nx, ny):
    own = SH_DEV * Q
    rows, surface = total.shape
    chunks, count = users.shape
    wide = count * Q
    row = row_ids((rows, wide))
    owner = row // own % nx * ny + row // (own * nx)
    target = owner * own + row % own
    expand = row_ids((count, wide)) == lane_ids((count, wide)) // Q
    expand = jnp.where(expand, f32(1.0), f32(0.0)).astype(bf16)

    def chunk_sum(i):
        ids = users[pl.ds(i, 1), :]
        both = jnp.concatenate([ids // 256, ids % 256], axis=0)
        both = jnp.concatenate([both, both, both, both], axis=0)
        place = jnp.dot(
            both.astype(f32).astype(bf16), expand, preferred_element_type=f32
        ).astype(jnp.int32)
        place = (place[0:1] * 256 + place[1:2]) * Q + lane_ids((1, wide)) % Q
        hot = jnp.where(target == place, f32(1.0), f32(0.0)).astype(bf16)
        block = child[:, pl.ds(pl.multiple_of(i * wide, wide), wide)]
        return lax.dot_general(
            hot, block, (((1,), (1,)), ((), ())), preferred_element_type=f32
        )

    total[...] = chunk_sum(0)
    if chunks > 1:

        def step(i, carry):
            total[...] += chunk_sum(i)
            return carry

        lax.fori_loop(1, chunks, step, 0)
    message = nx * own
    half = message // 2
    whole = surface // LANES
    tail = surface - whole * LANES
    for k in range(ny):
        block = total[k * message : (k + 1) * message, :]
        for c in range(whole):
            send[k, c * message : (c + 1) * message, :] = block[:, c * LANES : (c + 1) * LANES]
        if tail:
            gap = jnp.zeros((half, LANES // 2 - tail), f32)
            end = block[:, whole * LANES :]
            send[k, whole * message :, :] = jnp.concatenate(
                [end[:half], gap, end[half:], gap], axis=1
            )


def fused_kernel(
    nx,
    ny,
    live_in,
    child_in,
    users_in,
    local_in,
    pos_in,
    charge_in,
    nbrs_in,
    lists_in,
    ops_in,
    window,
    out,
    inner,
    lists,
    ops,
    live,
    child,
    users,
    local,
    pos,
    charge,
    nbrs,
    sums,
    send1,
    recv1,
    send2,
    recv2,
    recv3,
    spread,
    first,
    last,
    low,
    high,
    pos_low,
    pos_high,
    charge_low,
    charge_high,
    coords,
    charges,
    sources,
    targets,
    counts,
    gathered,
    load_sem,
    send_sem,
    recv_sem,
):
    mx, my = lax.axis_index("gx"), lax.axis_index("gy")
    total = nx * ny
    me = mx * ny + my
    has_low = me > 0
    has_high = me < total - 1

    def place(rank):
        return rank // ny, lax.rem(rank, ny)

    after = place(lax.rem(me + 1, total))
    before = place(lax.rem(me + total - 1, total))
    along_y = [(mx, lax.rem(my + d, ny)) for d in range(1, ny)]
    along_x = [(lax.rem(mx + d, nx), my) for d in range(1, nx)]

    barrier = pltpu.get_barrier_semaphore()

    def greet(device):
        pl.semaphore_signal(barrier, inc=1, device_id=device, device_id_type=MESH)

    for device in along_x + along_y:
        greet(device)
    pl.when(has_low)(lambda: greet(before))
    pl.when(has_high)(lambda: greet(after))

    def load(k, src, dst):
        copy = pltpu.make_async_copy(src, dst, load_sem.at[k])
        copy.start()
        return copy

    load_child = [load(0, child_in, child), load(1, users_in, users)]
    load_leaf = [load(2, pos_in, pos), load(3, charge_in, charge), load(4, nbrs_in, nbrs)]

    surface, wide = local.shape
    slots = wide // Q
    rim = low.shape[1]
    halo = pos_low.shape[1]
    count = pos.shape[1]
    own = SH_DEV * Q
    message = nx * own
    for copy in load_child:
        copy.wait()
    partial_sums(child, users, sums, send1, nx, ny)
    load_local = [load(5, local_in, local), load(6, live_in, live)]
    load_ops = [load(7, lists_in, lists), load(8, ops_in, ops)]

    def prepare():
        coords[...] = jnp.zeros_like(coords)
        coords[0:3, halo : halo + count] = pos[...]
        charges[:, halo : halo + count] = charge[...]
        mine = coords[:, halo : halo + count]
        sources[halo : halo + count, :] = source_rows(mine).T
        targets[...] = target_rows(mine)
        near_counts(nbrs[...], counts)

    for copy in load_leaf:
        copy.wait()
    groups = counts.shape[0]
    skip = halo // (GROUP * NPT)
    quads = (groups - 2 * skip) // 4

    def step(p, carry):
        for g in range(4):
            near_group(skip + 4 * p + g, sources, targets, charges, counts, out)
        return carry

    early = me < ny + 1

    def ahead():
        prepare()
        step(0, 0)

    def middle():
        for copy in load_local:
            copy.wait()
        last[...] = local[:, wide - rim :]
        first[...] = local[:, 0:rim]
        alive = alive_lanes(live[...], slots, (surface, wide))
        owned = jnp.where(alive, local[...].astype(f32), f32(0.0))
        window[:, rim : rim + wide] = owned.astype(bf16)
        for copy in load_ops:
            copy.wait()
        blocks = slots // BLOCK
        size = BLOCK * Q
        m2l_gather(window, lists[...], gathered, range(1, blocks - 1))
        value = jnp.dot(ops[...], gathered[...], preferred_element_type=f32)
        inner[...] = jnp.where(alive[:, size : wide - size], value, f32(0.0))

    pl.when(early)(ahead)
    pl.when(me == 0)(middle)
    neighbours = jnp.where(has_low, 1, 0) + jnp.where(has_high, 1, 0)
    pl.semaphore_wait(barrier, len(along_y) + len(along_x) + neighbours)

    at = [0]

    def remote(src, dst, device, sends=None, takes=None):
        k = at[0]
        at[0] += 1
        copy = pltpu.make_async_remote_copy(
            src_ref=src,
            dst_ref=dst,
            send_sem=send_sem.at[k],
            recv_sem=recv_sem.at[k],
            device_id=device,
            device_id_type=MESH,
        )
        if sends is None:
            copy.start()
            return copy.wait
        pl.when(sends)(copy.start)

        def wait():
            pl.when(sends)(copy.wait_send)
            pl.when(takes)(copy.wait_recv)

        return wait

    step1 = []
    for d in range(1, ny):
        step1.append(remote(send1.at[lax.rem(my + d, ny)], recv1.at[d - 1], along_y[d - 1]))
    leaf = [
        remote(pos.at[:, count - halo : count], pos_low, after, has_high, has_low),
        remote(charge.at[:, count - halo : count], charge_low, after, has_high, has_low),
        remote(pos.at[:, 0:halo], pos_high, before, has_low, has_high),
        remote(charge.at[:, 0:halo], charge_high, before, has_low, has_high),
    ]
    pl.when(jnp.logical_not(early))(ahead)
    pl.when(me > 0)(middle)
    half = jnp.where(me < 2, quads, jnp.where(early, jnp.minimum(2, quads), 1))
    lax.fori_loop(1, half, step, 0)

    for wait in step1:
        wait()
    value = send1[my]
    for d in range(ny - 1):
        value = value + recv1[d]
    value = unpack(value, message, surface)
    for k in range(nx):
        send2[k] = value[k * own : (k + 1) * own]
    step2 = []
    for d in range(nx):
        row = lax.rem(mx + d, nx)
        rank = row * ny + my
        left = place(lax.rem(rank + total - 1, total))
        step2.append(remote(send2.at[row], recv3.at[d], left, rank > 0, has_high))
        if d > 0:
            step2.append(remote(send2.at[row], recv2.at[d - 1], along_x[d - 1]))

    rims = [
        remote(last, low, after, has_high, has_low),
        remote(first, high, before, has_low, has_high),
    ]

    lax.fori_loop(half, quads, step, 0)

    lanes = spread.shape[0]
    alive = alive_lanes(live[...], slots, (surface, lanes))

    for wait in leaf:
        wait()
    for pos_ref, charge_ref, start, there in (
        (pos_low, charge_low, 0, has_low),
        (pos_high, charge_high, halo + count, has_high),
    ):
        span = slice(start, start + halo)
        coords[0:3, span] = jnp.where(there, pos_ref[...], f32(0.0))
        charges[:, span] = jnp.where(there, charge_ref[...], f32(0.0))
        sources[span, :] = source_rows(coords[:, span]).T

    for g in list(range(skip)) + list(range(groups - skip, groups)):
        near_group(g, sources, targets, charges, counts, out)

    for wait in rims:
        wait()
    window[:, 0:rim] = jnp.where(has_low, low[...], jnp.zeros_like(low))
    for wait in step2:
        wait()
    shared = send2[mx]
    for d in range(nx - 1):
        shared = shared + recv2[d]
    spread[...] = jnp.zeros_like(spread)
    spread[0:own, :] = shared
    front = local[:, 0:lanes].astype(f32) + spread[...].T
    front = jnp.where(alive, front, f32(0.0)).astype(bf16)
    window[:, rim : rim + lanes] = front
    shared = recv3[0]
    for d in range(1, nx):
        shared = shared + recv3[d]
    spread[0:own, :] = shared
    front = high[...].astype(f32) + spread[...].T[:, 0:rim]
    window[:, rim + wide :] = jnp.where(has_high, front, f32(0.0)).astype(bf16)


def fused(live, child, users, local, pos, charge, nbrs, lists, ops):
    nx, ny = lax.axis_size("gx"), lax.axis_size("gy")
    users = users.reshape(-1, 64)
    nbrs = nbrs.T
    live = live.reshape(1, 1)
    surface, wide = local.shape
    count = pos.shape[1]
    halo = HL * NPT
    groups = count // NPT // GROUP
    span = count + 2 * halo
    reach = (GROUP + 2 * HL) * NPT
    rim = wide // 16
    own = SH_DEV * Q
    packed = packed_rows(nx * own, surface)
    copies = ny - 1 + 2 * nx - 1 + 6
    vmem = pl.BlockSpec(memory_space=pltpu.VMEM)
    inputs = (live, child, users, local, pos, charge, nbrs, lists, ops)
    inputs = [live] + [pltpu.with_memory_space_constraint(x, pltpu.HBM) for x in inputs[1:]]
    return pl.pallas_call(
        functools.partial(fused_kernel, nx, ny),
        out_shape=(
            jax.ShapeDtypeStruct((surface, wide + 2 * rim), bf16),
            jax.ShapeDtypeStruct(charge.shape, f32),
            jax.ShapeDtypeStruct((surface, wide - 2 * BLOCK * Q), f32),
            jax.ShapeDtypeStruct(lists.shape, lists.dtype),
            jax.ShapeDtypeStruct(ops.shape, ops.dtype),
        ),
        in_specs=[pl.BlockSpec(memory_space=pltpu.HBM)] * len(inputs),
        out_specs=(vmem,) * 5,
        scratch_shapes=[pltpu.VMEM(x.shape, x.dtype) for x in inputs[:7]]
        + [
            pltpu.VMEM((ny * nx * own, surface), f32),
            pltpu.VMEM((ny, packed, LANES), f32),
            pltpu.VMEM((ny - 1, packed, LANES), f32),
            pltpu.VMEM((nx, own, surface), f32),
            pltpu.VMEM((nx - 1, own, surface), f32),
            pltpu.VMEM((nx, own, surface), f32),
            pltpu.VMEM((128, surface), f32),
            pltpu.VMEM((surface, rim), bf16),
            pltpu.VMEM((surface, rim), bf16),
            pltpu.VMEM((surface, rim), bf16),
            pltpu.VMEM((surface, rim), bf16),
            pltpu.VMEM((3, halo), f32),
            pltpu.VMEM((3, halo), f32),
            pltpu.VMEM((Q, halo), f32),
            pltpu.VMEM((Q, halo), f32),
            pltpu.VMEM((8, span), f32),
            pltpu.VMEM((Q, span), f32),
            pltpu.VMEM((span, 64), bf16),
            pltpu.VMEM((64, count), bf16),
            pltpu.VMEM((groups, GROUP, reach), f32),
            pltpu.VMEM((surface * lists.shape[0], wide - 2 * BLOCK * Q), bf16),
            pltpu.SemaphoreType.DMA((len(inputs),)),
            pltpu.SemaphoreType.DMA((copies,)),
            pltpu.SemaphoreType.DMA((copies,)),
        ],
        compiler_params=pltpu.CompilerParams(
            collective_id=0, has_side_effects=True, vmem_limit_bytes=32 * 2**20
        ),
    )(*inputs)


def m2l_kernel(live, window, lists, ops, near, inner, out, near_out, gathered, result, sem):
    surface, wide = out.shape
    size = BLOCK * Q
    copies = []

    def write(src, dst):
        copy = pltpu.make_async_copy(src, dst, sem.at[len(copies)])
        copy.start()
        copies.append(copy)

    write(inner, out.at[:, size : wide - size])
    write(near, near_out)
    m2l_gather(window, lists[...], gathered, (0, lists.shape[1] // BLOCK - 1))
    alive = alive_lanes(live[...], lists.shape[1], (surface, wide))
    value = jnp.dot(ops[...], gathered[...], preferred_element_type=f32)
    for part, start in ((slice(0, size), 0), (slice(size, 2 * size), wide - size)):
        span = slice(start, start + size)
        result[:, part] = jnp.where(alive[:, span], value[:, part], f32(0.0))
        write(result.at[:, part], out.at[:, span])
    for copy in copies:
        copy.wait()


def m2l(live, window, lists, ops, near, inner):
    surface = window.shape[0]
    wide = lists.shape[1] * Q
    size = BLOCK * Q
    vmem = pl.BlockSpec(memory_space=pltpu.VMEM)
    hbm = pl.BlockSpec(memory_space=pltpu.HBM)
    return pl.pallas_call(
        m2l_kernel,
        out_shape=(
            jax.ShapeDtypeStruct((surface, wide), f32),
            jax.ShapeDtypeStruct(near.shape, f32),
        ),
        in_specs=[vmem] * 6,
        out_specs=(hbm, hbm),
        scratch_shapes=[
            pltpu.VMEM((surface * lists.shape[0], 2 * size), bf16),
            pltpu.VMEM((surface, 2 * size), f32),
            pltpu.SemaphoreType.DMA((4,)),
        ],
        compiler_params=pltpu.CompilerParams(vmem_limit_bytes=24 * 2**20),
    )(live.reshape(1, 1), window, lists, ops, near, inner)


def per_device(
    child_dens, users, local_dens, live, m2l_ops, m2l_lists, leaf_pos, leaf_charge, leaf_nbrs
):
    window, near_pot, inner, lists, ops = fused(
        live, child_dens, users, local_dens, leaf_pos, leaf_charge, leaf_nbrs, m2l_lists, m2l_ops
    )
    return m2l(live, window, lists, ops, near_pot, inner)


def solution(mesh):
    placed = (
        P(None, ("gx", "gy")),
        P(("gx", "gy")),
        P(None, ("gx", "gy")),
        P(("gx", "gy")),
        P(),
        P(None, ("gx", "gy")),
        P(None, ("gx", "gy")),
        P(None, ("gx", "gy")),
        P(("gx", "gy"), None),
    )
    return jax.shard_map(
        per_device,
        mesh=mesh,
        in_specs=placed,
        out_specs=(P(None, ("gx", "gy")), P(None, ("gx", "gy"))),
        check_vma=False,
    )
```

```python
import functools

import jax
import jax.numpy as jnp
from jax import lax
from jax.experimental import pallas as pl
from jax.experimental.pallas import tpu as pltpu
from jax.sharding import PartitionSpec as P

Q = 4
NOFF = 8
SH_DEV = 1
NPT = 32
HL = 16
GROUP = 8
BLOCK = 32
LANES = 128

soften = 0.01
f32 = jnp.float32
bf16 = jnp.bfloat16
MESH = pl.DeviceIdType.MESH


def split3(value):
    first = value.astype(bf16).astype(f32)
    rest = value - first
    second = rest.astype(bf16).astype(f32)
    return first, second, rest - second


def row_ids(shape):
    return lax.broadcasted_iota(jnp.int32, shape, 0)


def lane_ids(shape):
    return lax.broadcasted_iota(jnp.int32, shape, 1)


def with_norm(coords):
    norm = jnp.sum(coords * coords, axis=0, keepdims=True)
    return jnp.where(row_ids(coords.shape) == 3, norm, coords), norm


def source_rows(coords):
    value, _ = with_norm(coords)
    one, two, three = split3(value)
    flat = jnp.where(row_ids(value.shape) < 3, f32(1.0), f32(0.0))
    return jnp.concatenate(
        [one, two, three, one, two, one, flat, jnp.zeros_like(one)], axis=0
    ).astype(bf16)


def target_rows(coords):
    value, norm = with_norm(coords)
    one, two, three = split3(value)
    row = row_ids(value.shape)
    main = jnp.where(row < 3, -2.0 * one, jnp.where(row == 3, f32(1.0), f32(0.0)))
    second = jnp.where(row < 3, -2.0 * two, f32(0.0))
    third = jnp.where(row < 3, -2.0 * three, f32(0.0))
    part = split3(norm + soften)
    flat = jnp.where(
        row == 0,
        part[0],
        jnp.where(row == 1, part[1], jnp.where(row == 2, part[2], f32(0.0))),
    )
    return jnp.concatenate(
        [main, main, main, second, second, third, flat, jnp.zeros_like(one)], axis=0
    ).astype(bf16)


def near_counts(nbrs, counts):
    slots, leaves = nbrs.shape
    groups, eight, reach = counts.shape
    span = GROUP + 2 * HL
    rows = -(-span // 16) * 16
    base = nbrs - lane_ids(nbrs.shape) // GROUP * GROUP
    base = jnp.where(nbrs < 0, -1, base)
    ids = row_ids((rows, leaves))
    total = jnp.zeros((rows, leaves), f32)
    for j in range(slots):
        total = total + jnp.where(ids == base[j : j + 1, :], f32(1.0), f32(0.0))
    spread = row_ids((rows, reach)) == lane_ids((rows, reach)) // NPT
    full = lax.dot_general(
        total.T.astype(bf16),
        jnp.where(spread, f32(1.0), f32(0.0)).astype(bf16),
        (((1,), (0,)), ((), ())),
        preferred_element_type=f32,
    )
    counts[...] = full.reshape(groups, eight, reach)


def near_group(g, sources, targets, charges, counts, out):
    reach = counts.shape[2]
    size = GROUP * NPT
    rows = Q * GROUP
    start = pl.multiple_of(g * size, size)
    right = targets[:, pl.ds(start, size)]
    cnt = counts[g]
    ch = charges[:, pl.ds(start, reach)]
    w = jnp.concatenate([cnt * ch[q : q + 1] for q in range(Q)], axis=0)
    wh = w.astype(bf16)
    wl = (w - wh.astype(f32)).astype(bf16)
    w = jnp.concatenate([wh, wl], axis=0)
    total = jnp.zeros((2 * rows, size), f32)
    rest = jnp.zeros((rows, size), f32)
    for at in range(0, reach, 256):
        width = min(256, reach - at)
        left = sources[pl.ds(pl.multiple_of(start + at, size), width), :]
        kernel = lax.rsqrt(jnp.dot(left, right, preferred_element_type=f32))
        high = kernel.astype(bf16)
        low = (kernel - high.astype(f32)).astype(bf16)
        span = slice(at, at + width)
        total = total + jnp.dot(w[:, span], high, preferred_element_type=f32)
        rest = rest + jnp.dot(wh[:, span], low, preferred_element_type=f32)
    flat = total[:rows] + total[rows:] + rest
    mine = row_ids(flat.shape) % GROUP == lane_ids(flat.shape) // NPT
    flat = jnp.where(mine, flat, f32(0.0))
    out[:, pl.ds(start, size)] = jnp.sum(flat.reshape(Q, GROUP, size), axis=1)


def alive_lanes(live, slots, shape):
    slot = lane_ids(shape) // Q
    lower = live // 2
    return (slot < lower) | (slot >= slots - (live - lower))


def m2l_gather(window, lists, gathered, blocks):
    offsets, slots = lists.shape
    surface = window.shape[0]
    wide = slots * Q
    expand = row_ids((slots, wide)) == lane_ids((slots, wide)) // Q
    place = jnp.dot(
        (lists + 1).astype(f32).astype(bf16),
        jnp.where(expand, f32(1.0), f32(0.0)).astype(bf16),
        preferred_element_type=f32,
    ).astype(jnp.int32)
    place = (place - 1) * Q + lane_ids(place.shape) % Q
    size = BLOCK * Q
    depth = (BLOCK + slots // 8) * Q
    for o in range(0, offsets, 2):
        for i, b in enumerate(blocks):
            block = window[:, b * size : b * size + depth]
            ids = row_ids((depth, size)) + b * size
            hits = [
                ids == place[k : k + 1, b * size : (b + 1) * size] for k in (o, o + 1)
            ]
            hot = jnp.concatenate([jnp.where(hit, f32(1.0), f32(0.0)) for hit in hits], axis=1)
            pair = jnp.dot(block, hot.astype(bf16), preferred_element_type=f32)
            both = jnp.concatenate([pair[:, :size], pair[:, size:]], axis=0).astype(bf16)
            gathered[o * surface : (o + 2) * surface, i * size : (i + 1) * size] = both


def packed_rows(message, surface):
    whole = surface // LANES
    tail = surface - whole * LANES
    assert tail <= LANES // 2
    return whole * message + (message // 2 if tail else 0)


def unpack(value, message, surface):
    whole = surface // LANES
    tail = surface - whole * LANES
    parts = [value[c * message : (c + 1) * message] for c in range(whole)]
    if tail:
        end = value[whole * message :]
        middle = LANES // 2
        parts.append(jnp.concatenate([end[:, :tail], end[:, middle : middle + tail]], axis=0))
    return jnp.concatenate(parts, axis=1)


def partial_sums(child, users, total, send, nx, ny):
    own = SH_DEV * Q
    rows, surface = total.shape
    chunks, count = users.shape
    wide = count * Q
    row = row_ids((rows, wide))
    owner = row // own % nx * ny + row // (own * nx)
    target = owner * own + row % own
    expand = row_ids((count, wide)) == lane_ids((count, wide)) // Q
    expand = jnp.where(expand, f32(1.0), f32(0.0)).astype(bf16)

    def chunk_sum(i):
        ids = users[pl.ds(i, 1), :]
        both = jnp.concatenate([ids // 256, ids % 256], axis=0)
        both = jnp.concatenate([both, both, both, both], axis=0)
        place = jnp.dot(
            both.astype(f32).astype(bf16), expand, preferred_element_type=f32
        ).astype(jnp.int32)
        place = (place[0:1] * 256 + place[1:2]) * Q + lane_ids((1, wide)) % Q
        hot = jnp.where(target == place, f32(1.0), f32(0.0)).astype(bf16)
        block = child[:, pl.ds(pl.multiple_of(i * wide, wide), wide)]
        return lax.dot_general(
            hot, block, (((1,), (1,)), ((), ())), preferred_element_type=f32
        )

    total[...] = chunk_sum(0)
    if chunks > 1:

        def step(i, carry):
            total[...] += chunk_sum(i)
            return carry

        lax.fori_loop(1, chunks, step, 0)
    message = nx * own
    half = message // 2
    whole = surface // LANES
    tail = surface - whole * LANES
    for k in range(ny):
        block = total[k * message : (k + 1) * message, :]
        for c in range(whole):
            send[k, c * message : (c + 1) * message, :] = block[:, c * LANES : (c + 1) * LANES]
        if tail:
            gap = jnp.zeros((half, LANES // 2 - tail), f32)
            end = block[:, whole * LANES :]
            send[k, whole * message :, :] = jnp.concatenate(
                [end[:half], gap, end[half:], gap], axis=1
            )


def fused_kernel(
    nx,
    ny,
    live_in,
    child_in,
    users_in,
    local_in,
    pos_in,
    charge_in,
    nbrs_in,
    lists_in,
    ops_in,
    window,
    out,
    inner,
    lists,
    ops,
    live,
    child,
    users,
    local,
    pos,
    charge,
    nbrs,
    sums,
    send1,
    recv1,
    send2,
    recv2,
    recv3,
    spread,
    first,
    last,
    low,
    high,
    pos_low,
    pos_high,
    charge_low,
    charge_high,
    coords,
    charges,
    sources,
    targets,
    counts,
    gathered,
    load_sem,
    send_sem,
    recv_sem,
):
    mx, my = lax.axis_index("gx"), lax.axis_index("gy")
    total = nx * ny
    me = mx * ny + my
    has_low = me > 0
    has_high = me < total - 1

    def place(rank):
        return rank // ny, lax.rem(rank, ny)

    after = place(lax.rem(me + 1, total))
    before = place(lax.rem(me + total - 1, total))
    along_y = [(mx, lax.rem(my + d, ny)) for d in range(1, ny)]
    along_x = [(lax.rem(mx + d, nx), my) for d in range(1, nx)]

    barrier = pltpu.get_barrier_semaphore()

    def greet(device):
        pl.semaphore_signal(barrier, inc=1, device_id=device, device_id_type=MESH)

    for device in along_x + along_y:
        greet(device)
    pl.when(has_low)(lambda: greet(before))
    pl.when(has_high)(lambda: greet(after))

    def load(k, src, dst):
        copy = pltpu.make_async_copy(src, dst, load_sem.at[k])
        copy.start()
        return copy

    load_child = [load(0, child_in, child), load(1, users_in, users)]
    load_leaf = [load(2, pos_in, pos), load(3, charge_in, charge), load(4, nbrs_in, nbrs)]

    surface, wide = local.shape
    slots = wide // Q
    rim = low.shape[0]
    lanes = spread.shape[0]
    halo = pos_low.shape[1]
    count = pos.shape[1]
    own = SH_DEV * Q
    message = nx * own
    for copy in load_child:
        copy.wait()
    partial_sums(child, users, sums, send1, nx, ny)
    load_local = [load(5, local_in, local), load(6, live_in, live)]
    load_ops = [load(7, lists_in, lists), load(8, ops_in, ops)]

    def prepare():
        coords[...] = jnp.zeros_like(coords)
        coords[0:3, halo : halo + count] = pos[...]
        charges[:, halo : halo + count] = charge[...]
        mine = coords[:, halo : halo + count]
        sources[halo : halo + count, :] = source_rows(mine).T
        targets[...] = target_rows(mine)
        near_counts(nbrs[...], counts)

    for copy in load_leaf:
        copy.wait()
    groups = counts.shape[0]
    skip = halo // (GROUP * NPT)
    quads = (groups - 2 * skip) // 4

    def step(p, carry):
        for g in range(4):
            near_group(skip + 4 * p + g, sources, targets, charges, counts, out)
        return carry

    early = me < 2 * ny
    late = me >= 2 * ny

    def ahead():
        prepare()
        step(0, 0)

    def middle():
        for copy in load_local:
            copy.wait()
        side = local[:, 0:lanes].astype(f32).T
        first[...] = side[0:rim].astype(bf16)
        side = local[:, wide - lanes :].astype(f32).T
        last[...] = side[lanes - rim :].astype(bf16)
        alive = alive_lanes(live[...], slots, (surface, wide))
        owned = jnp.where(alive, local[...].astype(f32), f32(0.0))
        window[:, 0:rim] = jnp.zeros((surface, rim), bf16)
        window[:, rim : rim + wide] = owned.astype(bf16)
        for copy in load_ops:
            copy.wait()
        blocks = slots // BLOCK
        m2l_gather(window, lists[...], gathered, range(1, blocks - 1))

    def product():
        size = BLOCK * Q
        alive = alive_lanes(live[...], slots, (surface, wide))
        value = jnp.dot(ops[...], gathered[...], preferred_element_type=f32)
        inner[...] = jnp.where(alive[:, size : wide - size], value, f32(0.0))

    pl.when(early)(ahead)
    pl.when(me == 0)(middle)
    pl.when(me == 0)(product)
    neighbours = jnp.where(has_low, 1, 0) + jnp.where(has_high, 1, 0)
    pl.semaphore_wait(barrier, len(along_y) + len(along_x) + neighbours)

    at = [0]

    def remote(src, dst, device, sends=None, takes=None, held=None):
        k = at[0]
        at[0] += 1
        copy = pltpu.make_async_remote_copy(
            src_ref=src,
            dst_ref=dst,
            send_sem=send_sem.at[k],
            recv_sem=recv_sem.at[k],
            device_id=device,
            device_id_type=MESH,
        )
        if sends is None:
            copy.start()
            return copy.wait
        if held is None:
            pl.when(sends)(copy.start)
        else:
            held.append((sends, copy))

        def wait():
            pl.when(sends)(copy.wait_send)
            pl.when(takes)(copy.wait_recv)

        return wait

    step1 = []
    for d in range(1, ny):
        step1.append(remote(send1.at[lax.rem(my + d, ny)], recv1.at[d - 1], along_y[d - 1]))
    pl.when(late)(ahead)
    pl.when(me > 0)(middle)
    pl.when(jnp.logical_and(me > 0, early))(product)
    held = []
    leaf = [
        remote(pos.at[:, count - halo : count], pos_low, after, has_high, has_low, held),
        remote(charge.at[:, count - halo : count], charge_low, after, has_high, has_low, held),
        remote(pos.at[:, 0:halo], pos_high, before, has_low, has_high, held),
        remote(charge.at[:, 0:halo], charge_high, before, has_low, has_high, held),
    ]
    rims = [
        remote(last, low, after, has_high, has_low, held),
        remote(first, high, before, has_low, has_high, held),
    ]
    soon = [early] * len(leaf) + [me < ny] * len(rims)
    for (sends, copy), first_turn in zip(held, soon):
        pl.when(jnp.logical_and(sends, first_turn))(copy.start)
    half = jnp.where(me < 2, quads, jnp.where(early, jnp.minimum(2, quads), 1))
    lax.fori_loop(1, half, step, 0)

    for wait in step1:
        wait()
    value = send1[my]
    for d in range(ny - 1):
        value = value + recv1[d]
    value = unpack(value, message, surface)
    for k in range(nx):
        send2[k] = value[k * own : (k + 1) * own]
    step2 = []
    for d in range(nx):
        row = lax.rem(mx + d, nx)
        rank = row * ny + my
        left = place(lax.rem(rank + total - 1, total))
        step2.append(remote(send2.at[row], recv3.at[d], left, rank > 0, has_high))
        if d > 0:
            step2.append(remote(send2.at[row], recv2.at[d - 1], along_x[d - 1]))

    for (sends, copy), first_turn in zip(held, soon):
        pl.when(jnp.logical_and(sends, jnp.logical_not(first_turn)))(copy.start)
    pl.when(late)(product)

    lax.fori_loop(half, quads, step, 0)

    for wait in leaf:
        wait()
    for pos_ref, charge_ref, start, there in (
        (pos_low, charge_low, 0, has_low),
        (pos_high, charge_high, halo + count, has_high),
    ):
        span = slice(start, start + halo)
        coords[0:3, span] = jnp.where(there, pos_ref[...], f32(0.0))
        charges[:, span] = jnp.where(there, charge_ref[...], f32(0.0))
        sources[span, :] = source_rows(coords[:, span]).T

    for g in list(range(skip)) + list(range(groups - skip, groups)):
        near_group(g, sources, targets, charges, counts, out)

    for wait in rims:
        wait()
    spread[...] = jnp.zeros_like(spread)
    spread[0:rim, :] = jnp.where(has_low, low[...].astype(f32), f32(0.0))
    top = lanes - rim
    spread[top:, :] = jnp.where(has_high, high[...].astype(f32), f32(0.0))
    slot = row_ids((own, surface)) // Q
    lower = live[...] // 2
    alive = (slot < lower) | (slot >= slots - (live[...] - lower))
    for wait in step2:
        wait()
    shared = send2[mx]
    for d in range(nx - 1):
        shared = shared + recv2[d]
    spread[rim : rim + own, :] = jnp.where(alive, shared, f32(0.0))
    shared = recv3[0]
    for d in range(1, nx):
        shared = shared + recv3[d]
    shared = spread[top : top + own, :] + shared
    spread[top : top + own, :] = jnp.where(has_high, shared, f32(0.0))
    turned = spread[...].T
    front = lane_ids(turned.shape) < top
    front = window[:, 0:lanes].astype(f32) + jnp.where(front, turned, f32(0.0))
    window[:, 0:lanes] = front.astype(bf16)
    window[:, rim + wide :] = turned[:, top:].astype(bf16)


def fused(live, child, users, local, pos, charge, nbrs, lists, ops):
    nx, ny = lax.axis_size("gx"), lax.axis_size("gy")
    users = users.reshape(-1, 64)
    nbrs = nbrs.T
    live = live.reshape(1, 1)
    surface, wide = local.shape
    count = pos.shape[1]
    halo = HL * NPT
    groups = count // NPT // GROUP
    span = count + 2 * halo
    reach = (GROUP + 2 * HL) * NPT
    rim = wide // 16
    own = SH_DEV * Q
    packed = packed_rows(nx * own, surface)
    copies = ny - 1 + 2 * nx - 1 + 6
    vmem = pl.BlockSpec(memory_space=pltpu.VMEM)
    inputs = (live, child, users, local, pos, charge, nbrs, lists, ops)
    inputs = [live] + [pltpu.with_memory_space_constraint(x, pltpu.HBM) for x in inputs[1:]]
    return pl.pallas_call(
        functools.partial(fused_kernel, nx, ny),
        out_shape=(
            jax.ShapeDtypeStruct((surface, wide + 2 * rim), bf16),
            jax.ShapeDtypeStruct(charge.shape, f32),
            jax.ShapeDtypeStruct((surface, wide - 2 * BLOCK * Q), f32),
            jax.ShapeDtypeStruct(lists.shape, lists.dtype),
            jax.ShapeDtypeStruct(ops.shape, ops.dtype),
        ),
        in_specs=[pl.BlockSpec(memory_space=pltpu.HBM)] * len(inputs),
        out_specs=(vmem,) * 5,
        scratch_shapes=[pltpu.VMEM(x.shape, x.dtype) for x in inputs[:7]]
        + [
            pltpu.VMEM((ny * nx * own, surface), f32),
            pltpu.VMEM((ny, packed, LANES), f32),
            pltpu.VMEM((ny - 1, packed, LANES), f32),
            pltpu.VMEM((nx, own, surface), f32),
            pltpu.VMEM((nx - 1, own, surface), f32),
            pltpu.VMEM((nx, own, surface), f32),
            pltpu.VMEM((128, surface), f32),
            pltpu.VMEM((rim, surface), bf16),
            pltpu.VMEM((rim, surface), bf16),
            pltpu.VMEM((rim, surface), bf16),
            pltpu.VMEM((rim, surface), bf16),
            pltpu.VMEM((3, halo), f32),
            pltpu.VMEM((3, halo), f32),
            pltpu.VMEM((Q, halo), f32),
            pltpu.VMEM((Q, halo), f32),
            pltpu.VMEM((8, span), f32),
            pltpu.VMEM((Q, span), f32),
            pltpu.VMEM((span, 64), bf16),
            pltpu.VMEM((64, count), bf16),
            pltpu.VMEM((groups, GROUP, reach), f32),
            pltpu.VMEM((surface * lists.shape[0], wide - 2 * BLOCK * Q), bf16),
            pltpu.SemaphoreType.DMA((len(inputs),)),
            pltpu.SemaphoreType.DMA((copies,)),
            pltpu.SemaphoreType.DMA((copies,)),
        ],
        compiler_params=pltpu.CompilerParams(
            collective_id=0, has_side_effects=True, vmem_limit_bytes=32 * 2**20
        ),
    )(*inputs)


def m2l_kernel(live, window, lists, ops, near, inner, out, near_out, gathered, result, sem):
    surface, wide = out.shape
    size = BLOCK * Q
    copies = []

    def write(src, dst):
        copy = pltpu.make_async_copy(src, dst, sem.at[len(copies)])
        copy.start()
        copies.append(copy)

    write(inner, out.at[:, size : wide - size])
    write(near, near_out)
    m2l_gather(window, lists[...], gathered, (0, lists.shape[1] // BLOCK - 1))
    alive = alive_lanes(live[...], lists.shape[1], (surface, wide))
    value = jnp.dot(ops[...], gathered[...], preferred_element_type=f32)
    for part, start in ((slice(0, size), 0), (slice(size, 2 * size), wide - size)):
        span = slice(start, start + size)
        result[:, part] = jnp.where(alive[:, span], value[:, part], f32(0.0))
        write(result.at[:, part], out.at[:, span])
    for copy in copies:
        copy.wait()


def m2l(live, window, lists, ops, near, inner):
    surface = window.shape[0]
    wide = lists.shape[1] * Q
    size = BLOCK * Q
    vmem = pl.BlockSpec(memory_space=pltpu.VMEM)
    hbm = pl.BlockSpec(memory_space=pltpu.HBM)
    return pl.pallas_call(
        m2l_kernel,
        out_shape=(
            jax.ShapeDtypeStruct((surface, wide), f32),
            jax.ShapeDtypeStruct(near.shape, f32),
        ),
        in_specs=[vmem] * 6,
        out_specs=(hbm, hbm),
        scratch_shapes=[
            pltpu.VMEM((surface * lists.shape[0], 2 * size), bf16),
            pltpu.VMEM((surface, 2 * size), f32),
            pltpu.SemaphoreType.DMA((4,)),
        ],
        compiler_params=pltpu.CompilerParams(vmem_limit_bytes=24 * 2**20),
    )(live.reshape(1, 1), window, lists, ops, near, inner)


def per_device(
    child_dens, users, local_dens, live, m2l_ops, m2l_lists, leaf_pos, leaf_charge, leaf_nbrs
):
    window, near_pot, inner, lists, ops = fused(
        live, child_dens, users, local_dens, leaf_pos, leaf_charge, leaf_nbrs, m2l_lists, m2l_ops
    )
    return m2l(live, window, lists, ops, near_pot, inner)


def solution(mesh):
    placed = (
        P(None, ("gx", "gy")),
        P(("gx", "gy")),
        P(None, ("gx", "gy")),
        P(("gx", "gy")),
        P(),
        P(None, ("gx", "gy")),
        P(None, ("gx", "gy")),
        P(None, ("gx", "gy")),
        P(("gx", "gy"), None),
    )
    return jax.shard_map(
        per_device,
        mesh=mesh,
        in_specs=placed,
        out_specs=(P(None, ("gx", "gy")), P(None, ("gx", "gy"))),
        check_vma=False,
    )
```

```python
import functools

import jax
import jax.numpy as jnp
from jax import lax
from jax.experimental import pallas as pl
from jax.experimental.pallas import tpu as pltpu
from jax.sharding import PartitionSpec as P

Q = 4
NOFF = 8
SH_DEV = 1
NPT = 32
HL = 16
GROUP = 8
BLOCK = 32
LANES = 128

soften = 0.01
f32 = jnp.float32
bf16 = jnp.bfloat16
MESH = pl.DeviceIdType.MESH


def split3(value):
    first = value.astype(bf16).astype(f32)
    rest = value - first
    second = rest.astype(bf16).astype(f32)
    return first, second, rest - second


def row_ids(shape):
    return lax.broadcasted_iota(jnp.int32, shape, 0)


def lane_ids(shape):
    return lax.broadcasted_iota(jnp.int32, shape, 1)


def with_norm(coords):
    norm = jnp.sum(coords * coords, axis=0, keepdims=True)
    return jnp.where(row_ids(coords.shape) == 3, norm, coords), norm


def source_rows(coords):
    value, _ = with_norm(coords)
    one, two, three = split3(value)
    flat = jnp.where(row_ids(value.shape) < 3, f32(1.0), f32(0.0))
    return jnp.concatenate(
        [one, two, three, one, two, one, flat, jnp.zeros_like(one)], axis=0
    ).astype(bf16)


def target_rows(coords):
    value, norm = with_norm(coords)
    one, two, three = split3(value)
    row = row_ids(value.shape)
    main = jnp.where(row < 3, -2.0 * one, jnp.where(row == 3, f32(1.0), f32(0.0)))
    second = jnp.where(row < 3, -2.0 * two, f32(0.0))
    third = jnp.where(row < 3, -2.0 * three, f32(0.0))
    part = split3(norm + soften)
    flat = jnp.where(
        row == 0,
        part[0],
        jnp.where(row == 1, part[1], jnp.where(row == 2, part[2], f32(0.0))),
    )
    return jnp.concatenate(
        [main, main, main, second, second, third, flat, jnp.zeros_like(one)], axis=0
    ).astype(bf16)


def near_counts(nbrs, counts):
    slots, leaves = nbrs.shape
    groups, eight, reach = counts.shape
    span = GROUP + 2 * HL
    rows = -(-span // 16) * 16
    base = nbrs - lane_ids(nbrs.shape) // GROUP * GROUP
    base = jnp.where(nbrs < 0, -1, base)
    ids = row_ids((rows, leaves))
    total = jnp.zeros((rows, leaves), f32)
    for j in range(slots):
        total = total + jnp.where(ids == base[j : j + 1, :], f32(1.0), f32(0.0))
    spread = row_ids((rows, reach)) == lane_ids((rows, reach)) // NPT
    full = lax.dot_general(
        total.T.astype(bf16),
        jnp.where(spread, f32(1.0), f32(0.0)).astype(bf16),
        (((1,), (0,)), ((), ())),
        preferred_element_type=f32,
    )
    counts[...] = full.reshape(groups, eight, reach)


def near_group(g, sources, targets, charges, counts, out):
    reach = counts.shape[2]
    size = GROUP * NPT
    rows = Q * GROUP
    start = pl.multiple_of(g * size, size)
    right = targets[:, pl.ds(start, size)]
    cnt = counts[g]
    ch = charges[:, pl.ds(start, reach)]
    w = jnp.concatenate([cnt * ch[q : q + 1] for q in range(Q)], axis=0)
    wh = w.astype(bf16)
    wl = (w - wh.astype(f32)).astype(bf16)
    w = jnp.concatenate([wh, wl], axis=0)
    total = jnp.zeros((2 * rows, size), f32)
    rest = jnp.zeros((rows, size), f32)
    for at in range(0, reach, 256):
        width = min(256, reach - at)
        left = sources[pl.ds(pl.multiple_of(start + at, size), width), :]
        kernel = lax.rsqrt(jnp.dot(left, right, preferred_element_type=f32))
        high = kernel.astype(bf16)
        low = (kernel - high.astype(f32)).astype(bf16)
        span = slice(at, at + width)
        total = total + jnp.dot(w[:, span], high, preferred_element_type=f32)
        rest = rest + jnp.dot(wh[:, span], low, preferred_element_type=f32)
    flat = total[:rows] + total[rows:] + rest
    mine = row_ids(flat.shape) % GROUP == lane_ids(flat.shape) // NPT
    flat = jnp.where(mine, flat, f32(0.0))
    out[:, pl.ds(start, size)] = jnp.sum(flat.reshape(Q, GROUP, size), axis=1)


def alive_lanes(live, slots, shape):
    slot = lane_ids(shape) // Q
    lower = live // 2
    return (slot < lower) | (slot >= slots - (live - lower))


def m2l_gather(window, lists, gathered, blocks):
    offsets, slots = lists.shape
    surface = window.shape[0]
    wide = slots * Q
    expand = row_ids((slots, wide)) == lane_ids((slots, wide)) // Q
    place = jnp.dot(
        (lists + 1).astype(f32).astype(bf16),
        jnp.where(expand, f32(1.0), f32(0.0)).astype(bf16),
        preferred_element_type=f32,
    ).astype(jnp.int32)
    place = (place - 1) * Q + lane_ids(place.shape) % Q
    size = BLOCK * Q
    depth = (BLOCK + slots // 8) * Q
    for o in range(0, offsets, 2):
        for i, b in enumerate(blocks):
            block = window[:, b * size : b * size + depth]
            ids = row_ids((depth, size)) + b * size
            hits = [
                ids == place[k : k + 1, b * size : (b + 1) * size] for k in (o, o + 1)
            ]
            hot = jnp.concatenate([jnp.where(hit, f32(1.0), f32(0.0)) for hit in hits], axis=1)
            pair = jnp.dot(block, hot.astype(bf16), preferred_element_type=f32)
            both = jnp.concatenate([pair[:, :size], pair[:, size:]], axis=0).astype(bf16)
            gathered[o * surface : (o + 2) * surface, i * size : (i + 1) * size] = both


def packed_rows(message, surface):
    whole = surface // LANES
    tail = surface - whole * LANES
    assert tail <= LANES // 2
    return whole * message + (message // 2 if tail else 0)


def unpack(value, message, surface):
    whole = surface // LANES
    tail = surface - whole * LANES
    parts = [value[c * message : (c + 1) * message] for c in range(whole)]
    if tail:
        end = value[whole * message :]
        middle = LANES // 2
        parts.append(jnp.concatenate([end[:, :tail], end[:, middle : middle + tail]], axis=0))
    return jnp.concatenate(parts, axis=1)


def partial_sums(child, users, total, send, nx, ny):
    own = SH_DEV * Q
    rows, surface = total.shape
    chunks, count = users.shape
    wide = count * Q
    row = row_ids((rows, wide))
    owner = row // own % nx * ny + row // (own * nx)
    target = owner * own + row % own
    expand = row_ids((count, wide)) == lane_ids((count, wide)) // Q
    expand = jnp.where(expand, f32(1.0), f32(0.0)).astype(bf16)

    def chunk_sum(i):
        ids = users[pl.ds(i, 1), :]
        both = jnp.concatenate([ids // 256, ids % 256], axis=0)
        both = jnp.concatenate([both, both, both, both], axis=0)
        place = jnp.dot(
            both.astype(f32).astype(bf16), expand, preferred_element_type=f32
        ).astype(jnp.int32)
        place = (place[0:1] * 256 + place[1:2]) * Q + lane_ids((1, wide)) % Q
        hot = jnp.where(target == place, f32(1.0), f32(0.0)).astype(bf16)
        block = child[:, pl.ds(pl.multiple_of(i * wide, wide), wide)]
        return lax.dot_general(
            hot, block, (((1,), (1,)), ((), ())), preferred_element_type=f32
        )

    total[...] = chunk_sum(0)
    if chunks > 1:

        def step(i, carry):
            total[...] += chunk_sum(i)
            return carry

        lax.fori_loop(1, chunks, step, 0)
    message = nx * own
    half = message // 2
    whole = surface // LANES
    tail = surface - whole * LANES
    for k in range(ny):
        block = total[k * message : (k + 1) * message, :]
        for c in range(whole):
            send[k, c * message : (c + 1) * message, :] = block[:, c * LANES : (c + 1) * LANES]
        if tail:
            gap = jnp.zeros((half, LANES // 2 - tail), f32)
            end = block[:, whole * LANES :]
            send[k, whole * message :, :] = jnp.concatenate(
                [end[:half], gap, end[half:], gap], axis=1
            )


def fused_kernel(
    nx,
    ny,
    live_in,
    child_in,
    users_in,
    local_in,
    pos_in,
    charge_in,
    nbrs_in,
    lists_in,
    ops_in,
    window,
    out,
    inner,
    lists,
    ops,
    live,
    child,
    users,
    local,
    pos,
    charge,
    nbrs,
    sums,
    send1,
    recv1,
    send2,
    recv2,
    recv3,
    spread,
    first,
    last,
    low,
    high,
    pos_low,
    pos_high,
    charge_low,
    charge_high,
    coords,
    charges,
    sources,
    targets,
    counts,
    gathered,
    load_sem,
    send_sem,
    recv_sem,
):
    mx, my = lax.axis_index("gx"), lax.axis_index("gy")
    total = nx * ny
    me = mx * ny + my
    has_low = me > 0
    has_high = me < total - 1

    def place(rank):
        return rank // ny, lax.rem(rank, ny)

    after = place(lax.rem(me + 1, total))
    before = place(lax.rem(me + total - 1, total))
    along_y = [(mx, lax.rem(my + d, ny)) for d in range(1, ny)]
    along_x = [(lax.rem(mx + d, nx), my) for d in range(1, nx)]

    barrier = pltpu.get_barrier_semaphore()

    def greet(device):
        pl.semaphore_signal(barrier, inc=1, device_id=device, device_id_type=MESH)

    for device in along_x + along_y:
        greet(device)
    pl.when(has_low)(lambda: greet(before))
    pl.when(has_high)(lambda: greet(after))

    def load(k, src, dst):
        copy = pltpu.make_async_copy(src, dst, load_sem.at[k])
        copy.start()
        return copy

    load_child = [load(0, child_in, child), load(1, users_in, users)]
    load_leaf = [load(2, pos_in, pos), load(3, charge_in, charge), load(4, nbrs_in, nbrs)]

    surface, wide = local.shape
    slots = wide // Q
    rim = low.shape[0]
    lanes = spread.shape[0]
    halo = pos_low.shape[1]
    count = pos.shape[1]
    own = SH_DEV * Q
    message = nx * own
    for copy in load_child:
        copy.wait()
    partial_sums(child, users, sums, send1, nx, ny)
    load_local = [load(5, local_in, local), load(6, live_in, live)]
    load_ops = [load(7, lists_in, lists), load(8, ops_in, ops)]

    def prepare():
        coords[...] = jnp.zeros_like(coords)
        coords[0:3, halo : halo + count] = pos[...]
        charges[:, halo : halo + count] = charge[...]
        mine = coords[:, halo : halo + count]
        sources[halo : halo + count, :] = source_rows(mine).T
        targets[...] = target_rows(mine)
        near_counts(nbrs[...], counts)

    for copy in load_leaf:
        copy.wait()
    groups = counts.shape[0]
    skip = halo // (GROUP * NPT)
    quads = (groups - 2 * skip) // 4

    def step(p, carry):
        for g in range(4):
            near_group(skip + 4 * p + g, sources, targets, charges, counts, out)
        return carry

    early = me < 2 * ny
    late = me >= 2 * ny
    final = me >= jnp.maximum(2, nx - 1) * ny

    def ahead():
        prepare()
        step(0, 0)

    def middle():
        for copy in load_local:
            copy.wait()
        side = local[:, 0:lanes].astype(f32).T
        first[...] = side[0:rim].astype(bf16)
        side = local[:, wide - lanes :].astype(f32).T
        last[...] = side[lanes - rim :].astype(bf16)
        alive = alive_lanes(live[...], slots, (surface, wide))
        owned = jnp.where(alive, local[...].astype(f32), f32(0.0))
        window[:, 0:rim] = jnp.zeros((surface, rim), bf16)
        window[:, rim : rim + wide] = owned.astype(bf16)
        for copy in load_ops:
            copy.wait()
        blocks = slots // BLOCK
        m2l_gather(window, lists[...], gathered, range(1, blocks - 1))

    def product():
        size = BLOCK * Q
        alive = alive_lanes(live[...], slots, (surface, wide))
        value = jnp.dot(ops[...], gathered[...], preferred_element_type=f32)
        inner[...] = jnp.where(alive[:, size : wide - size], value, f32(0.0))

    pl.when(early)(ahead)
    pl.when(me == 0)(middle)
    pl.when(me == 0)(product)
    pl.when(jnp.logical_and(late, jnp.logical_not(final)))(prepare)
    neighbours = jnp.where(has_low, 1, 0) + jnp.where(has_high, 1, 0)
    pl.semaphore_wait(barrier, len(along_y) + len(along_x) + neighbours)

    at = [0]

    def remote(src, dst, device, sends=None, takes=None, held=None):
        k = at[0]
        at[0] += 1
        copy = pltpu.make_async_remote_copy(
            src_ref=src,
            dst_ref=dst,
            send_sem=send_sem.at[k],
            recv_sem=recv_sem.at[k],
            device_id=device,
            device_id_type=MESH,
        )
        if sends is None:
            copy.start()
            return copy.wait
        if held is None:
            pl.when(sends)(copy.start)
        else:
            held.append((sends, copy))

        def wait():
            pl.when(sends)(copy.wait_send)
            pl.when(takes)(copy.wait_recv)

        return wait

    step1 = []
    for d in range(1, ny):
        step1.append(remote(send1.at[lax.rem(my + d, ny)], recv1.at[d - 1], along_y[d - 1]))
    pl.when(final)(prepare)
    lax.fori_loop(0, jnp.where(late, 1, 0), step, 0)
    pl.when(me > 0)(middle)
    pl.when(me > 0)(product)
    held = []
    leaf = [
        remote(pos.at[:, count - halo : count], pos_low, after, has_high, has_low, held),
        remote(charge.at[:, count - halo : count], charge_low, after, has_high, has_low, held),
        remote(pos.at[:, 0:halo], pos_high, before, has_low, has_high, held),
        remote(charge.at[:, 0:halo], charge_high, before, has_low, has_high, held),
    ]
    rims = [
        remote(last, low, after, has_high, has_low, held),
        remote(first, high, before, has_low, has_high, held),
    ]
    soon = [early] * len(leaf) + [me < ny] * len(rims)
    for (sends, copy), first_turn in zip(held, soon):
        pl.when(jnp.logical_and(sends, first_turn))(copy.start)
    half = jnp.where(me < 2, quads, jnp.where(early, jnp.minimum(2, quads), 1))
    lax.fori_loop(1, half, step, 0)

    for wait in step1:
        wait()
    value = send1[my]
    for d in range(ny - 1):
        value = value + recv1[d]
    value = unpack(value, message, surface)
    for k in range(nx):
        send2[k] = value[k * own : (k + 1) * own]
    step2 = []
    for d in range(nx):
        row = lax.rem(mx + d, nx)
        rank = row * ny + my
        left = place(lax.rem(rank + total - 1, total))
        step2.append(remote(send2.at[row], recv3.at[d], left, rank > 0, has_high))
        if d > 0:
            step2.append(remote(send2.at[row], recv2.at[d - 1], along_x[d - 1]))

    for (sends, copy), first_turn in zip(held, soon):
        pl.when(jnp.logical_and(sends, jnp.logical_not(first_turn)))(copy.start)

    lax.fori_loop(half, quads, step, 0)

    for wait in leaf:
        wait()
    for pos_ref, charge_ref, start, there in (
        (pos_low, charge_low, 0, has_low),
        (pos_high, charge_high, halo + count, has_high),
    ):
        span = slice(start, start + halo)
        coords[0:3, span] = jnp.where(there, pos_ref[...], f32(0.0))
        charges[:, span] = jnp.where(there, charge_ref[...], f32(0.0))
        sources[span, :] = source_rows(coords[:, span]).T

    for g in list(range(skip)) + list(range(groups - skip, groups)):
        near_group(g, sources, targets, charges, counts, out)

    for wait in rims:
        wait()
    spread[...] = jnp.zeros_like(spread)
    spread[0:rim, :] = jnp.where(has_low, low[...].astype(f32), f32(0.0))
    top = lanes - rim
    spread[top:, :] = jnp.where(has_high, high[...].astype(f32), f32(0.0))
    slot = row_ids((own, surface)) // Q
    lower = live[...] // 2
    alive = (slot < lower) | (slot >= slots - (live[...] - lower))
    for wait in step2:
        wait()
    shared = send2[mx]
    for d in range(nx - 1):
        shared = shared + recv2[d]
    spread[rim : rim + own, :] = jnp.where(alive, shared, f32(0.0))
    shared = recv3[0]
    for d in range(1, nx):
        shared = shared + recv3[d]
    shared = spread[top : top + own, :] + shared
    spread[top : top + own, :] = jnp.where(has_high, shared, f32(0.0))
    turned = spread[...].T
    front = lane_ids(turned.shape) < top
    front = window[:, 0:lanes].astype(f32) + jnp.where(front, turned, f32(0.0))
    window[:, 0:lanes] = front.astype(bf16)
    window[:, rim + wide :] = turned[:, top:].astype(bf16)


def fused(live, child, users, local, pos, charge, nbrs, lists, ops):
    nx, ny = lax.axis_size("gx"), lax.axis_size("gy")
    users = users.reshape(-1, 64)
    nbrs = nbrs.T
    live = live.reshape(1, 1)
    surface, wide = local.shape
    count = pos.shape[1]
    halo = HL * NPT
    groups = count // NPT // GROUP
    span = count + 2 * halo
    reach = (GROUP + 2 * HL) * NPT
    rim = wide // 16
    own = SH_DEV * Q
    packed = packed_rows(nx * own, surface)
    copies = ny - 1 + 2 * nx - 1 + 6
    vmem = pl.BlockSpec(memory_space=pltpu.VMEM)
    inputs = (live, child, users, local, pos, charge, nbrs, lists, ops)
    inputs = [live] + [pltpu.with_memory_space_constraint(x, pltpu.HBM) for x in inputs[1:]]
    return pl.pallas_call(
        functools.partial(fused_kernel, nx, ny),
        out_shape=(
            jax.ShapeDtypeStruct((surface, wide + 2 * rim), bf16),
            jax.ShapeDtypeStruct(charge.shape, f32),
            jax.ShapeDtypeStruct((surface, wide - 2 * BLOCK * Q), f32),
            jax.ShapeDtypeStruct(lists.shape, lists.dtype),
            jax.ShapeDtypeStruct(ops.shape, ops.dtype),
        ),
        in_specs=[pl.BlockSpec(memory_space=pltpu.HBM)] * len(inputs),
        out_specs=(vmem,) * 5,
        scratch_shapes=[pltpu.VMEM(x.shape, x.dtype) for x in inputs[:7]]
        + [
            pltpu.VMEM((ny * nx * own, surface), f32),
            pltpu.VMEM((ny, packed, LANES), f32),
            pltpu.VMEM((ny - 1, packed, LANES), f32),
            pltpu.VMEM((nx, own, surface), f32),
            pltpu.VMEM((nx - 1, own, surface), f32),
            pltpu.VMEM((nx, own, surface), f32),
            pltpu.VMEM((128, surface), f32),
            pltpu.VMEM((rim, surface), bf16),
            pltpu.VMEM((rim, surface), bf16),
            pltpu.VMEM((rim, surface), bf16),
            pltpu.VMEM((rim, surface), bf16),
            pltpu.VMEM((3, halo), f32),
            pltpu.VMEM((3, halo), f32),
            pltpu.VMEM((Q, halo), f32),
            pltpu.VMEM((Q, halo), f32),
            pltpu.VMEM((8, span), f32),
            pltpu.VMEM((Q, span), f32),
            pltpu.VMEM((span, 64), bf16),
            pltpu.VMEM((64, count), bf16),
            pltpu.VMEM((groups, GROUP, reach), f32),
            pltpu.VMEM((surface * lists.shape[0], wide - 2 * BLOCK * Q), bf16),
            pltpu.SemaphoreType.DMA((len(inputs),)),
            pltpu.SemaphoreType.DMA((copies,)),
            pltpu.SemaphoreType.DMA((copies,)),
        ],
        compiler_params=pltpu.CompilerParams(
            collective_id=0, has_side_effects=True, vmem_limit_bytes=32 * 2**20
        ),
    )(*inputs)


def m2l_kernel(live, window, lists, ops, near, inner, out, near_out, gathered, result, sem):
    surface, wide = out.shape
    size = BLOCK * Q
    copies = []

    def write(src, dst):
        copy = pltpu.make_async_copy(src, dst, sem.at[len(copies)])
        copy.start()
        copies.append(copy)

    write(inner, out.at[:, size : wide - size])
    write(near, near_out)
    m2l_gather(window, lists[...], gathered, (0, lists.shape[1] // BLOCK - 1))
    alive = alive_lanes(live[...], lists.shape[1], (surface, wide))
    value = jnp.dot(ops[...], gathered[...], preferred_element_type=f32)
    for part, start in ((slice(0, size), 0), (slice(size, 2 * size), wide - size)):
        span = slice(start, start + size)
        result[:, part] = jnp.where(alive[:, span], value[:, part], f32(0.0))
        write(result.at[:, part], out.at[:, span])
    for copy in copies:
        copy.wait()


def m2l(live, window, lists, ops, near, inner):
    surface = window.shape[0]
    wide = lists.shape[1] * Q
    size = BLOCK * Q
    vmem = pl.BlockSpec(memory_space=pltpu.VMEM)
    hbm = pl.BlockSpec(memory_space=pltpu.HBM)
    return pl.pallas_call(
        m2l_kernel,
        out_shape=(
            jax.ShapeDtypeStruct((surface, wide), f32),
            jax.ShapeDtypeStruct(near.shape, f32),
        ),
        in_specs=[vmem] * 6,
        out_specs=(hbm, hbm),
        scratch_shapes=[
            pltpu.VMEM((surface * lists.shape[0], 2 * size), bf16),
            pltpu.VMEM((surface, 2 * size), f32),
            pltpu.SemaphoreType.DMA((4,)),
        ],
        compiler_params=pltpu.CompilerParams(vmem_limit_bytes=24 * 2**20),
    )(live.reshape(1, 1), window, lists, ops, near, inner)


def per_device(
    child_dens, users, local_dens, live, m2l_ops, m2l_lists, leaf_pos, leaf_charge, leaf_nbrs
):
    window, near_pot, inner, lists, ops = fused(
        live, child_dens, users, local_dens, leaf_pos, leaf_charge, leaf_nbrs, m2l_lists, m2l_ops
    )
    return m2l(live, window, lists, ops, near_pot, inner)


def solution(mesh):
    placed = (
        P(None, ("gx", "gy")),
        P(("gx", "gy")),
        P(None, ("gx", "gy")),
        P(("gx", "gy")),
        P(),
        P(None, ("gx", "gy")),
        P(None, ("gx", "gy")),
        P(None, ("gx", "gy")),
        P(("gx", "gy"), None),
    )
    return jax.shard_map(
        per_device,
        mesh=mesh,
        in_specs=placed,
        out_specs=(P(None, ("gx", "gy")), P(None, ("gx", "gy"))),
        check_vma=False,
    )
```
